32 devices in a mesh: layer: 4 (over y, x), feat: 8 (over z, core).
Axes of the slice: x: 2, y: 2, z: 4, core: 2. Of those that a mesh axis runs over, the one named last changes fastest.
Arguments:
- acts: bfloat16 [4, 256, 8192], P(None, 'layer', 'feat'), may hold values from -6 to 6
- layer_order: int32 [4, 4], P('layer'), may hold values from 0 to 3, each once within a row
- groups: int32 [8192], P('feat'), may hold values from 0 to 63
- group_scale: float32 [4, 64], P('layer'), may hold values from 0.25 to 4
- shrink: float32 [4], P('layer'), may hold values from 0.1 to 0.6
Outputs:
- factor_tiles: float32 [4, 8, 4, 1024, 1024], P('layer', 'feat')
- far_tiles: float32 [4, 8, 512, 1024], P('layer', 'feat')
The draws below stay inside these ranges and needn't reach their ends.
Inputs may be any that keep to these rules, and one draw needn't show every extreme that they name: Each row of layer_order names every layer once.
All inputs are finite; a program needn't handle non-finite values.
Results may differ from the reference program's by a relative error of at most 0.0003.
Values may be sent and summed in bfloat16 or wider, within the bound.
No kernel may reach another device: no remote copies, remote signals or barrier semaphores. Data moves between devices by JAX's collectives and lax.ppermute only.
A program may use at most 64 MiB of HBM per device.

```python
import math
import jax
import jax.numpy as jnp
from jax import lax

D = 8192
TOK_DEV = 64
GROUPS = 64
LAYERS = 4
SOURCES = 4
TOKENS = 256
PANELS = 8
PANEL = 1024
HALF = 4


def touch_ends(result, rng, low, top_value):
    longest = result.shape.index(max(result.shape))
    spots = []
    for shift in (0, 1):
        where = [jax.random.randint(jax.random.fold_in(rng, axis), (), 0, length) for axis, length in enumerate(result.shape)]
        where[longest] = (where[longest] + shift) % result.shape[longest]
        spots.append(tuple(where))
    return result.at[spots[0]].set(low).at[spots[1]].set(top_value)


def level_of(rng, shape, pieces, least, high):
    level, own = 1.0, jax.random.fold_in(rng, 6)
    for dim, shards_of in pieces:
        heights = jnp.exp(jax.random.uniform(jax.random.fold_in(own, dim), (shards_of,), jnp.float32, least / len(pieces), high / len(pieces)))
        level = level * jnp.repeat(heights, shape[dim] // shards_of).reshape([-1 if axis == dim else 1 for axis in range(len(shape))])
    return level


def noise(own_key, shape, width, bound, shards=(), held_as=jnp.bfloat16):
    level = level_of(own_key, shape, shards, -0.22, 0.18) if shards else 1.0
    result = jax.random.normal(own_key, shape, jnp.float32) * width * level
    return jnp.minimum(jnp.maximum(result, -bound), bound).astype(held_as)


def setup_inputs(seed: int = 0) -> dict:
    arg_keys = jax.random.split(jax.random.key(seed), 6)
    return {
        "acts": noise(arg_keys[0], (LAYERS, TOKENS, D), 1.0, 6.0, ((1, 4), (2, 8))),
        "layer_order": jax.vmap(lambda own: jax.random.permutation(own, LAYERS))(jax.random.split(arg_keys[1], SOURCES)).reshape((SOURCES, LAYERS)).astype(jnp.int32),
        "groups": touch_ends(jax.random.randint(arg_keys[2], (D,), 0, GROUPS), jax.random.fold_in(arg_keys[2], 1), 0, GROUPS - 1).astype(jnp.int32),
        "group_scale": jnp.clip(jnp.exp(math.log(4.0) - 2.7725887 * jax.random.uniform(arg_keys[3], (LAYERS, GROUPS), jnp.float32) ** level_of(arg_keys[3], (LAYERS, GROUPS), ((0, 4),), -0.2, 0.2)), 0.25, 4.0),
        "shrink": jnp.clip(0.1 + 0.5 * jax.random.uniform(arg_keys[4], (LAYERS,), jnp.float32) ** level_of(arg_keys[4], (LAYERS,), ((0, 4),), -0.2, 0.2), 0.1, 0.6),
    }


def reference(acts, layer_order, groups, group_scale, shrink):
    sources = layer_order.shape[0]
    blocks = acts.reshape(LAYERS, sources, TOK_DEV, D)
    hits = (layer_order[:, None, :] == jnp.arange(LAYERS, dtype=jnp.int32)[None, :, None]).astype(jnp.int32)
    slot = jnp.sum(hits * jnp.arange(LAYERS, dtype=jnp.int32)[None, None, :], axis=2).astype(jnp.int32)
    source_ids = jnp.arange(sources, dtype=jnp.int32)[:, None]
    picked = blocks[slot, source_ids]
    by_layer = jnp.transpose(picked, (1, 0, 2, 3)).reshape(LAYERS, TOKENS, D)
    panel_ids = jnp.arange(PANELS, dtype=jnp.int32)
    offsets = jnp.arange(HALF, dtype=jnp.int32)
    columns = ((panel_ids[:, None] + offsets[None, :]) % PANELS).astype(jnp.int32)
    first = jnp.arange(HALF, dtype=jnp.int32)
    identity = jnp.eye(PANEL, dtype=jnp.float32)

    def one_layer(inputs):
        rows, gains, weight = inputs
        wide = rows.astype(jnp.float32)
        gram = jnp.dot(wide.T, wide, precision=lax.Precision.HIGHEST) / TOKENS
        mu = jnp.trace(gram) / D
        grid = gram.reshape(PANELS, PANEL, PANELS, PANEL).transpose(0, 2, 1, 3)
        tiles = grid[panel_ids[:, None], columns] * (1.0 - weight)
        diagonal = (weight * mu * gains[groups]).reshape(PANELS, PANEL)
        tiles = tiles.at[:, 0].add(diagonal[:, :, None] * identity[None])
        paired = grid[first, first + HALF]
        far = jnp.concatenate([paired[:, :PANEL // 2], paired[:, PANEL // 2:]], 0) * (1.0 - weight)
        return tiles, far

    factor_tiles, far_tiles = lax.map(one_layer, (by_layer, group_scale, shrink))
    return factor_tiles, far_tiles
```

```python
import jax
import jax.numpy as jnp
from jax import lax
from jax.experimental import pallas as pl
from jax.experimental.pallas import tpu as pltpu
from jax.sharding import PartitionSpec as P

TRANSPOSED = (((0,), (0,)), ((), ()))


def whole_block(shape):
    return pl.BlockSpec(shape, lambda *_: (0,) * len(shape))


def row_step(rows):
    step = min(rows, 256)
    while rows % step:
        step -= 8
    return step


def tile_kernel(count, has_diagonal, where_ref, scale_ref, own_ref, *rest):
    candidates, rest = rest[:count], rest[count:]
    diagonal_ref = rest[0] if has_diagonal else None
    out_ref, chosen = rest[-2:]
    step = pl.program_id(0)

    @pl.when(step == 0)
    def _():
        for i, candidate in enumerate(candidates):

            @pl.when(where_ref[1] == i)
            def _(candidate=candidate):
                chosen[...] = candidate[...]

    value = lax.dot_general(
        own_ref[...], chosen[...], TRANSPOSED, preferred_element_type=jnp.float32
    ) * scale_ref[0]
    if has_diagonal:
        rows = lax.broadcasted_iota(jnp.int32, value.shape, 0) + step * value.shape[0]
        columns = lax.broadcasted_iota(jnp.int32, value.shape, 1)
        value = value + jnp.where(rows == columns, diagonal_ref[...], 0.0)
    out_ref[0] = value


def tile(stack, index, own, candidates, pick, scale, count, diagonal=None):
    tokens, width = own.shape
    rows = row_step(width)
    where = jnp.stack([jnp.asarray(index, jnp.int32), jnp.asarray(pick, jnp.int32)])
    operands = [own, *candidates] + ([diagonal] if diagonal is not None else [])
    in_specs = [
        pl.BlockSpec(memory_space=pltpu.SMEM),
        pl.BlockSpec((tokens, rows), lambda i, w: (0, i)),
    ]
    in_specs += [whole_block(o.shape) for o in operands[1:]]
    aliases = {}
    if stack is not None:
        operands.append(stack)
        in_specs.append(pl.BlockSpec(memory_space=pl.ANY))
        aliases = {len(operands) + 1: 0}

    def body(where_ref, scale_ref, own_ref, *rest):
        if stack is not None:
            rest = rest[:-3] + rest[-2:]
        tile_kernel(len(candidates), diagonal is not None, where_ref, scale_ref, own_ref, *rest)

    return pl.pallas_call(
        body,
        out_shape=jax.ShapeDtypeStruct((count, width, width), jnp.float32),
        grid_spec=pltpu.PrefetchScalarGridSpec(
            num_scalar_prefetch=1,
            grid=(width // rows,),
            in_specs=in_specs,
            out_specs=pl.BlockSpec((1, rows, width), lambda i, w: (w[0], i, 0)),
            scratch_shapes=[pltpu.VMEM((tokens, width), own.dtype)],
        ),
        input_output_aliases=aliases,
        cost_estimate=pl.CostEstimate(
            flops=2 * tokens * width * width,
            bytes_accessed=4 * width * width + 2 * tokens * width * (1 + len(candidates)),
            transcendentals=0,
        ),
        name="gram_tile",
    )(where, scale, *operands)


def far_kernel(count, where_ref, scale_ref, own_ref, *rest):
    candidates, (out_ref, left, right) = rest[:count], rest[count:]
    rows = left.shape[1]

    @pl.when(where_ref[0] == 1)
    def _():
        left[...] = own_ref[:, :rows]

    @pl.when(where_ref[0] == 0)
    def _():
        right[...] = own_ref[...]

    for i, candidate in enumerate(candidates):

        @pl.when((where_ref[0] == 1) & (where_ref[1] == i))
        def _(candidate=candidate):
            right[...] = candidate[...]

        @pl.when((where_ref[0] == 0) & (where_ref[1] == i))
        def _(candidate=candidate):
            left[...] = candidate[:, rows:]

    out_ref[...] = lax.dot_general(
        left[...], right[...], TRANSPOSED, preferred_element_type=jnp.float32
    ) * scale_ref[0]


def far_tile(own, candidates, lower, pick, scale):
    tokens, width = own.shape
    rows = width // 2
    where = jnp.stack([lower.astype(jnp.int32), jnp.asarray(pick, jnp.int32)])

    def body(where_ref, scale_ref, own_ref, *rest):
        far_kernel(len(candidates), where_ref, scale_ref, own_ref, *rest)

    return pl.pallas_call(
        body,
        out_shape=jax.ShapeDtypeStruct((rows, width), jnp.float32),
        grid_spec=pltpu.PrefetchScalarGridSpec(
            num_scalar_prefetch=1,
            grid=(1,),
            in_specs=[pl.BlockSpec(memory_space=pltpu.SMEM)]
            + [whole_block(own.shape)] * (1 + len(candidates)),
            out_specs=whole_block((rows, width)),
            scratch_shapes=[
                pltpu.VMEM((tokens, rows), own.dtype),
                pltpu.VMEM((tokens, width), own.dtype),
            ],
        ),
        cost_estimate=pl.CostEstimate(
            flops=2 * tokens * rows * width,
            bytes_accessed=4 * rows * width + 2 * tokens * width * (1 + len(candidates)),
            transcendentals=0,
        ),
        name="far_tile",
    )(where, scale, own, *candidates)


def partners(count):
    if count & (count - 1):
        return [[(i + k) % count for i in range(count)] for k in range(1, count)]
    return [[i ^ k for i in range(count)] for k in range(1, count)]


def along(block, pairs, cores):
    return lax.ppermute(
        block, "feat", [(2 * s + c, 2 * d + c) for s, d in pairs for c in cores]
    )


def swapped(block, cores=(0, 1)):
    chips = lax.axis_size("feat") // 2
    return lax.ppermute(
        block, "feat", [(2 * z + c, 2 * z + 1 - c) for z in range(chips) for c in cores]
    )


def summed(value, axis):
    count = lax.axis_size(axis)
    if count & (count - 1):
        return lax.psum(value, axis)
    step = 1
    while step < count:
        value = value + lax.ppermute(value, axis, [(i, i ^ step) for i in range(count)])
        step *= 2
    return value


def shards(acts, layer_order, groups, group_scale, shrink):
    layers, _, width = acts.shape
    panels = lax.axis_size("feat")
    half = panels // 2
    chips = panels // 2
    reach = chips // 2
    here = lax.axis_index("layer")
    f = lax.axis_index("feat")
    z, core = f // 2, f % 2
    weight = shrink[0]

    def block_of(layer):
        slot = jnp.sum(
            jnp.where(layer_order[0] == layer, jnp.arange(layers, dtype=jnp.int32), 0)
        )
        return lax.dynamic_index_in_dim(acts, slot, 0, keepdims=False)

    blocks = [block_of(here)]
    for to in partners(layers):
        target = jnp.asarray(to, jnp.int32)[here]
        blocks.append(lax.ppermute(block_of(target), "layer", list(enumerate(to))))
    own = jnp.concatenate(blocks, 0)
    tokens = own.shape[0]
    scale = ((1.0 - weight) / tokens)[None]

    left = [own]
    for k in range(1, reach + 1):
        pairs = [(d + 1, d) for d in range(chips - k)]
        left.append(along(left[-1], pairs, (0, 1)))
    right = [along(own, [(s, s + reach) for s in range(reach)], (0, 1))]
    for m in range(1, reach):
        pairs = [(d - 1, d) for d in range(reach + m, chips)]
        right.append(along(right[-1], pairs, (0, 1)))

    squares = own.astype(jnp.float32)
    part = jnp.sum(squares * squares)
    mu = summed(jnp.full((8, 128), part, jnp.float32), "feat")[0, 0] / tokens
    mu = mu / (width * panels)
    members = (
        groups[None, :] == jnp.arange(group_scale.shape[1], dtype=jnp.int32)[:, None]
    ).astype(jnp.float32)
    gains = jnp.dot(group_scale, members, precision=lax.Precision.HIGHEST)
    diagonal = weight * mu * gains

    stack = tile(None, 0, own, [own], 0, scale, half, diagonal)
    for k in range(1, reach):
        pair = [left[k], right[reach - k]]
        pick = (z + k >= chips).astype(jnp.int32)
        stack = tile(stack, 2 * k, own, pair, pick, scale, half)
        ahead = jnp.where(pick == 0, pair[0], pair[1])
        other = swapped(ahead)
        index = jnp.where(core == 0, 2 * k + 1, 2 * k - 1)
        stack = tile(stack, index, own, [other], 0, scale, half)
    pair = [left[reach], right[0]]
    pick = (z + reach >= chips).astype(jnp.int32)
    far = jnp.where(pick == 0, pair[0], pair[1])
    other = swapped(jnp.where(core == 0, far, own))
    index = jnp.where(core == 0, 1, half - 1)
    stack = tile(stack, index, own, [other], 0, scale, half)
    far_out = far_tile(own, pair, f < half, pick, scale)
    return (stack[None, None], far_out[None, None])


def solution(mesh):
    placed = (P(None, "layer", "feat"), P("layer", None), P("feat"), P("layer", None), P("layer"))
    return jax.shard_map(
        shards,
        mesh=mesh,
        in_specs=placed,
        out_specs=(P("layer", "feat", None, None, None), P("layer", "feat", None, None)),
        check_vma=False,
    )
```

```python
import math

import jax
import jax.numpy as jnp
from jax import lax
from jax.experimental import pallas as pl
from jax.experimental.pallas import tpu as pltpu
from jax.sharding import PartitionSpec as P

TRANSPOSED = (((0,), (0,)), ((), ()))
SMEM = pl.BlockSpec(memory_space=pltpu.SMEM)
VMEM = pl.BlockSpec(memory_space=pltpu.VMEM)
HBM = pl.BlockSpec(memory_space=pltpu.HBM)
ANY = pl.BlockSpec(memory_space=pl.ANY)


def room(*shapes):
    total = sum(math.prod(shape) * jnp.dtype(dtype).itemsize for shape, dtype in shapes)
    return pltpu.CompilerParams(vmem_limit_bytes=total + (2 << 20))


def like(*arrays):
    return [(a.shape, a.dtype) for a in arrays]


def partner(i, k, count):
    return (i + k) % count if count & (count - 1) else i ^ k


def select(acts, layer_order):
    layers, rows, width = acts.shape

    def body(order_ref, acts_ref, *rest):
        outs, sem = rest[:-1], rest[-1]
        here = lax.axis_index("layer")
        copies = []
        for k in range(layers):
            layer = partner(here, k, layers)
            slot = jnp.int32(0)
            for s in range(1, layers):
                slot = jnp.where(order_ref[0, s] == layer, s, slot)
            copies.append(pltpu.make_async_copy(acts_ref.at[slot], outs[k], sem.at[k]))
            copies[-1].start()
        for copy in copies:
            copy.wait()

    return pl.pallas_call(
        body,
        out_shape=[jax.ShapeDtypeStruct((rows, width), acts.dtype)] * layers,
        in_specs=[SMEM, HBM],
        out_specs=[VMEM] * layers,
        scratch_shapes=[pltpu.SemaphoreType.DMA((layers,))],
        compiler_params=room(*like(acts)),
        name="select",
    )(layer_order, acts)


def gather(blocks):
    rows, width = blocks[0].shape
    tokens = rows * len(blocks)

    def body(*refs):
        parts, (own_ref, part_ref) = refs[:-2], refs[-2:]
        total = jnp.zeros((1, width), jnp.float32)
        for j, part in enumerate(parts):
            own_ref[j * rows : (j + 1) * rows, :] = part[...]
            value = part[...].astype(jnp.float32)
            total = total + jnp.sum(value * value, axis=0, keepdims=True)
        part_ref[...] = jnp.broadcast_to(jnp.sum(total) / tokens, part_ref.shape)

    return pl.pallas_call(
        body,
        out_shape=[
            jax.ShapeDtypeStruct((tokens, width), blocks[0].dtype),
            jax.ShapeDtypeStruct((8, 128), jnp.float32),
        ],
        in_specs=[VMEM] * len(blocks),
        out_specs=[VMEM] * 2,
        compiler_params=room(*like(*blocks) * 2),
        name="gather",
    )(*blocks)


def place():
    f = lax.axis_index("feat")
    return f, f // 2, f % 2


def assemble(panel_ref, blocks):
    start = 0
    for block in blocks:
        panel_ref[start : start + block.shape[0], :] = block[...]
        start += block.shape[0]


def handover(blocks, given):

    def body(*refs):
        parts, (given_ref, out_ref) = refs[:-2], refs[-2:]
        f, z, core = place()

        @pl.when(core == 0)
        def _():
            assemble(out_ref, parts)

        @pl.when(core != 0)
        def _():
            out_ref[...] = given_ref[...]

    return pl.pallas_call(
        body,
        out_shape=jax.ShapeDtypeStruct(given.shape, given.dtype),
        in_specs=[VMEM] * (len(blocks) + 1),
        out_specs=VMEM,
        compiler_params=room(*like(*blocks, given, given)),
        name="handover",
    )(*blocks, given)


def tile(stack, count, own, blocks, index, shrink, keep=False, diagonal=None):
    tokens, width = own.shape
    step = next(s for s in (128, 64, 32, 16, 8, width) if width % s == 0)
    steps = width // step
    extra = [] if diagonal is None else diagonal

    def body(shrink_ref, own_ref, *rest):
        parts, rest = rest[: len(blocks)], rest[len(blocks) :]
        added, rest = rest[: len(extra)], rest[len(extra) :]
        rest = rest[(stack is not None) :]
        out_ref, rest = rest[0], rest[1:]
        if keep:
            panel, rest = rest[0], rest[1:]
        else:
            panel, rest = rest[-1], rest[:-1]
        buffer, sem = rest
        f, z, core = place()
        to = index(core)
        assemble(panel, parts)
        scale = (1.0 - shrink_ref[0]) * (1.0 / tokens)
        if extra:
            gains_ref, sums = added[0], added[1:]
            trace = sums[0][0:1, 0:1]
            for other in sums[1:]:
                trace = trace + other[0:1, 0:1]
            mu = trace * (1.0 / (width * lax.axis_size("feat")))
            line = gains_ref[...] * (mu * shrink_ref[0])
        copies = []
        for i in range(steps):
            rows = slice(i * step, (i + 1) * step)
            value = (
                lax.dot_general(
                    own_ref[:, rows],
                    panel[...],
                    TRANSPOSED,
                    preferred_element_type=jnp.float32,
                )
                * scale
            )
            buffer[rows, :] = value
            if extra:
                shape = (step, step)
                same = lax.broadcasted_iota(jnp.int32, shape, 0) == lax.broadcasted_iota(
                    jnp.int32, shape, 1
                )
                buffer[rows, rows] = value[:, rows] + jnp.where(same, line[:, rows], 0.0)
            copies.append(
                pltpu.make_async_copy(buffer.at[rows, :], out_ref.at[to, rows, :], sem.at[i])
            )
            copies[-1].start()
        for copy in copies:
            copy.wait()

    out_shape = [jax.ShapeDtypeStruct((count, width, width), jnp.float32)]
    out_specs = [ANY]
    scratch = [pltpu.VMEM((width, width), jnp.float32), pltpu.SemaphoreType.DMA((steps,))]
    if keep:
        out_shape.append(jax.ShapeDtypeStruct((tokens, width), own.dtype))
        out_specs.append(VMEM)
    else:
        scratch.append(pltpu.VMEM((tokens, width), own.dtype))
    operands = [shrink, own, *blocks, *extra] + ([] if stack is None else [stack])
    in_specs = [SMEM] + [VMEM] * (1 + len(blocks) + len(extra)) + [ANY] * (stack is not None)
    outs = pl.pallas_call(
        body,
        out_shape=out_shape,
        in_specs=in_specs,
        out_specs=out_specs,
        scratch_shapes=scratch,
        input_output_aliases={} if stack is None else {len(operands) - 1: 0},
        compiler_params=room(*like(own, own, *blocks, *extra), ((width, width), jnp.float32)),
        cost_estimate=pl.CostEstimate(
            flops=2 * tokens * width * width,
            bytes_accessed=4 * width * width + 4 * tokens * width,
            transcendentals=0,
        ),
        name="gram_tile",
    )(*operands)
    return outs if keep else outs[0]


def far_tile(own, blocks, shrink):
    tokens, width = own.shape
    rows = width // 2

    def body(shrink_ref, own_ref, *rest):
        parts, (out_ref, left, panel) = rest[: len(blocks)], rest[len(blocks) :]
        f, z, core = place()
        lower = f < lax.axis_size("feat") // 2
        scale = (1.0 - shrink_ref[0]) * (1.0 / tokens)

        @pl.when(lower)
        def _():
            left[...] = own_ref[:, :rows]
            assemble(panel, parts)

        @pl.when(jnp.logical_not(lower))
        def _():
            assemble(panel, parts)
            left[...] = panel[:, rows:]
            panel[...] = own_ref[...]

        out_ref[...] = (
            lax.dot_general(left[...], panel[...], TRANSPOSED, preferred_element_type=jnp.float32)
            * scale
        )

    return pl.pallas_call(
        body,
        out_shape=jax.ShapeDtypeStruct((rows, width), jnp.float32),
        in_specs=[SMEM] + [VMEM] * (1 + len(blocks)),
        out_specs=VMEM,
        scratch_shapes=[
            pltpu.VMEM((tokens, rows), own.dtype),
            pltpu.VMEM((tokens, width), own.dtype),
        ],
        compiler_params=room(*like(own, own, own, *blocks), ((width, width), jnp.float32)),
        cost_estimate=pl.CostEstimate(
            flops=2 * tokens * rows * width,
            bytes_accessed=4 * rows * width + 4 * tokens * width,
            transcendentals=0,
        ),
        name="far_tile",
    )(shrink, own, *blocks)


def behind(block, k):
    count = lax.axis_size("feat")
    return lax.ppermute(block, "feat", [((i + 2 * k) % count, i) for i in range(count)])


def swapped(block):
    return lax.ppermute(block, "feat", [(i, i ^ 1) for i in range(lax.axis_size("feat"))])


def shards(acts, layer_order, groups, group_scale, shrink):
    layers, _, width = acts.shape
    half = lax.axis_size("feat") // 2
    chips = half
    reach = chips // 2

    sent = select(acts, layer_order)
    blocks = [sent[0]]
    for k in range(1, layers):
        route = [(i, partner(i, k, layers)) for i in range(layers)]
        blocks.append(lax.ppermute(sent[k], "layer", route))

    ahead = [blocks]
    for k in range(reach):
        ahead.append([behind(b, 1) for b in ahead[-1]])

    own, part = gather(blocks)
    part = part + swapped(part)
    sums = [part] + [behind(part, k) for k in range(1, chips)]
    members = (
        groups[None, :] == jnp.arange(group_scale.shape[1], dtype=jnp.int32)[:, None]
    ).astype(jnp.float32)
    gains = jnp.dot(group_scale, members, precision=lax.Precision.HIGHEST)

    stack = None
    for k in range(1, reach):
        stack, panel = tile(stack, half, own, ahead[k], lambda core, k=k: 2 * k, shrink, keep=True)
        index = lambda core, k=k: jnp.where(core == 0, 2 * k + 1, 2 * k - 1)
        stack = tile(stack, half, own, [swapped(panel)], index, shrink)
    stack = tile(stack, half, own, [own], lambda core: 0, shrink, diagonal=[gains, *sums])
    other = swapped(handover(ahead[reach], own))
    far = far_tile(own, ahead[reach], shrink)
    index = lambda core: jnp.where(core == 0, 1, half - 1)
    stack = tile(stack, half, own, [other], index, shrink)
    return (stack[None, None], far[None, None])


def solution(mesh):
    placed = (P(None, "layer", "feat"), P("layer", None), P("feat"), P("layer", None), P("layer"))
    return jax.shard_map(
        shards,
        mesh=mesh,
        in_specs=placed,
        out_specs=(P("layer", "feat", None, None, None), P("layer", "feat", None, None)),
        check_vma=False,
    )
```

```python
import math

import jax
import jax.numpy as jnp
from jax import lax
from jax.experimental import pallas as pl
from jax.experimental.pallas import tpu as pltpu
from jax.sharding import PartitionSpec as P

TRANSPOSED = (((0,), (0,)), ((), ()))
SMEM = pl.BlockSpec(memory_space=pltpu.SMEM)
VMEM = pl.BlockSpec(memory_space=pltpu.VMEM)
HBM = pl.BlockSpec(memory_space=pltpu.HBM)
ANY = pl.BlockSpec(memory_space=pl.ANY)


def room(*shapes):
    total = sum(math.prod(shape) * jnp.dtype(dtype).itemsize for shape, dtype in shapes)
    return pltpu.CompilerParams(vmem_limit_bytes=total + (2 << 20))


def like(*arrays):
    return [(a.shape, a.dtype) for a in arrays]


def partner(i, k, count):
    return (i + k) % count if count & (count - 1) else i ^ k


def select(acts, layer_order):
    layers, rows, width = acts.shape

    def body(order_ref, acts_ref, *rest):
        outs, (held, order, sem) = rest[:layers], rest[layers:]
        copies = [
            pltpu.make_async_copy(order_ref, order, sem.at[0]),
            pltpu.make_async_copy(acts_ref, held, sem.at[1]),
        ]
        for copy in copies:
            copy.start()
        here = lax.axis_index("layer")
        copies[0].wait()
        slots = []
        for k in range(layers):
            layer = partner(here, k, layers)
            slot = jnp.int32(0)
            for s in range(1, layers):
                slot = jnp.where(order[0, s] == layer, s, slot)
            slots.append(slot)
        copies[1].wait()
        for out, slot in zip(outs, slots):
            out[...] = held[slot]

    return pl.pallas_call(
        body,
        out_shape=[jax.ShapeDtypeStruct((rows, width), acts.dtype)] * layers,
        in_specs=[ANY, ANY],
        out_specs=[VMEM] * layers,
        scratch_shapes=[
            pltpu.VMEM(acts.shape, acts.dtype),
            pltpu.SMEM(layer_order.shape, layer_order.dtype),
            pltpu.SemaphoreType.DMA((2,)),
        ],
        name="select",
    )(layer_order, acts)


def prepare(block, groups, group_scale):
    count = group_scale.shape[1]

    def body(scale_ref, groups_ref, block_ref, out_ref, gains_ref):
        out_ref[...] = block_ref[...]
        line = jnp.zeros(groups_ref.shape, jnp.float32)
        for g in range(count):
            line = jnp.where(groups_ref[...] == g, scale_ref[0, g], line)
        gains_ref[...] = line

    return pl.pallas_call(
        body,
        out_shape=[
            jax.ShapeDtypeStruct(block.shape, block.dtype),
            jax.ShapeDtypeStruct((1, groups.shape[0]), jnp.float32),
        ],
        in_specs=[SMEM, VMEM, VMEM],
        out_specs=[VMEM] * 2,
        compiler_params=room(*like(block, block, groups, groups)),
        name="prepare",
    )(group_scale, groups[None], block)


def join(blocks):
    if len(blocks) == 1:
        return blocks[0]
    shape = (sum(b.shape[0] for b in blocks), blocks[0].shape[1])

    def body(*refs):
        assemble(refs[-1], refs[:-1])

    return pl.pallas_call(
        body,
        out_shape=jax.ShapeDtypeStruct(shape, blocks[0].dtype),
        in_specs=[VMEM] * len(blocks),
        out_specs=VMEM,
        compiler_params=room(*like(*blocks) * 2),
        name="join",
    )(*blocks)


def gather(blocks):
    rows, width = blocks[0].shape
    tokens = rows * len(blocks)

    def body(*refs):
        parts, (own_ref, part_ref) = refs[:-2], refs[-2:]
        total = jnp.zeros((1, width), jnp.float32)
        for j, part in enumerate(parts):
            own_ref[j * rows : (j + 1) * rows, :] = part[...]
            value = part[...].astype(jnp.float32)
            total = total + jnp.sum(value * value, axis=0, keepdims=True)
        part_ref[...] = jnp.broadcast_to(jnp.sum(total) / tokens, part_ref.shape)

    return pl.pallas_call(
        body,
        out_shape=[
            jax.ShapeDtypeStruct((tokens, width), blocks[0].dtype),
            jax.ShapeDtypeStruct((8, 128), jnp.float32),
        ],
        in_specs=[VMEM] * len(blocks),
        out_specs=[VMEM] * 2,
        compiler_params=room(*like(*blocks) * 2),
        name="gather",
    )(*blocks)


def place():
    f = lax.axis_index("feat")
    return f, f // 2, f % 2


def assemble(panel_ref, blocks):
    start = 0
    for block in blocks:
        panel_ref[start : start + block.shape[0], :] = block[...]
        start += block.shape[0]


def tile(stack, count, own, blocks, index, shrink, keep=False, diagonal=None, odd=()):
    tokens, width = own.shape
    step = next(s for s in (128, 64, 32, 16, 8, width) if width % s == 0)
    steps = width // step
    extra = [] if diagonal is None else diagonal
    given = [*blocks, *odd]

    def body(shrink_ref, own_ref, *rest):
        parts, rest = rest[: len(given)], rest[len(given) :]
        added, rest = rest[: len(extra)], rest[len(extra) :]
        rest = rest[(stack is not None) :]
        out_ref, rest = rest[0], rest[1:]
        if keep:
            panel, rest = rest[0], rest[1:]
        else:
            panel, rest = rest[-1], rest[:-1]
        buffer, sem = rest
        _, _, core = place()
        to = index(core)
        if odd:
            pl.when(core == 0)(lambda: assemble(panel, parts[: len(blocks)]))
            pl.when(core != 0)(lambda: assemble(panel, parts[len(blocks) :]))
        else:
            assemble(panel, parts)
        scale = (1.0 - shrink_ref[0]) * (1.0 / tokens)
        if extra:
            gains_ref, sums = added[0], added[1:]
            trace = sums[0][0:1, 0:1]
            for other in sums[1:]:
                trace = trace + other[0:1, 0:1]
            mu = trace * (1.0 / (width * lax.axis_size("feat")))
            line = gains_ref[...] * (mu * shrink_ref[0])
        copies = []
        for i in range(steps):
            rows = slice(i * step, (i + 1) * step)
            value = (
                lax.dot_general(
                    own_ref[:, rows],
                    panel[...],
                    TRANSPOSED,
                    preferred_element_type=jnp.float32,
                )
                * scale
            )
            buffer[rows, :] = value
            if extra:
                shape = (step, step)
                same = lax.broadcasted_iota(jnp.int32, shape, 0) == lax.broadcasted_iota(
                    jnp.int32, shape, 1
                )
                buffer[rows, rows] = value[:, rows] + jnp.where(same, line[:, rows], 0.0)
            copies.append(
                pltpu.make_async_copy(buffer.at[rows, :], out_ref.at[to, rows, :], sem.at[i])
            )
            copies[-1].start()
        for copy in copies:
            copy.wait()

    out_shape = [jax.ShapeDtypeStruct((count, width, width), jnp.float32)]
    out_specs = [ANY]
    scratch = [pltpu.VMEM((width, width), jnp.float32), pltpu.SemaphoreType.DMA((steps,))]
    if keep:
        out_shape.append(jax.ShapeDtypeStruct((tokens, width), own.dtype))
        out_specs.append(VMEM)
    else:
        scratch.append(pltpu.VMEM((tokens, width), own.dtype))
    operands = [shrink, own, *given, *extra] + ([] if stack is None else [stack])
    in_specs = [SMEM] + [VMEM] * (1 + len(given) + len(extra)) + [ANY] * (stack is not None)
    outs = pl.pallas_call(
        body,
        out_shape=out_shape,
        in_specs=in_specs,
        out_specs=out_specs,
        scratch_shapes=scratch,
        input_output_aliases={} if stack is None else {len(operands) - 1: 0},
        compiler_params=room(*like(own, own, *given, *extra), ((width, width), jnp.float32)),
        cost_estimate=pl.CostEstimate(
            flops=2 * tokens * width * width,
            bytes_accessed=4 * width * width + 4 * tokens * width,
            transcendentals=0,
        ),
        name="gram_tile",
    )(*operands)
    return outs if keep else outs[0]


def far_tile(own, blocks, shrink):
    tokens, width = own.shape
    rows = width // 2

    step = next(s for s in (128, 64, 32, 16, 8, rows) if rows % s == 0)
    steps = rows // step

    def body(shrink_ref, own_ref, *rest):
        parts, (out_ref, left, panel, buffer, sem) = rest[: len(blocks)], rest[len(blocks) :]
        f, _, _ = place()
        lower = f < lax.axis_size("feat") // 2
        scale = (1.0 - shrink_ref[0]) * (1.0 / tokens)
        assemble(panel, parts)

        @pl.when(lower)
        def _():
            left[...] = own_ref[:, :rows]

        @pl.when(jnp.logical_not(lower))
        def _():
            left[...] = panel[:, rows:]
            panel[...] = own_ref[...]

        copies = []
        for i in range(steps):
            part = slice(i * step, (i + 1) * step)
            buffer[part, :] = (
                lax.dot_general(
                    left[:, part],
                    panel[...],
                    TRANSPOSED,
                    preferred_element_type=jnp.float32,
                )
                * scale
            )
            copies.append(
                pltpu.make_async_copy(buffer.at[part, :], out_ref.at[part, :], sem.at[i])
            )
            copies[-1].start()
        for copy in copies:
            copy.wait()

    return pl.pallas_call(
        body,
        out_shape=jax.ShapeDtypeStruct((rows, width), jnp.float32),
        in_specs=[SMEM] + [VMEM] * (1 + len(blocks)),
        out_specs=ANY,
        scratch_shapes=[
            pltpu.VMEM((tokens, rows), own.dtype),
            pltpu.VMEM((tokens, width), own.dtype),
            pltpu.VMEM((rows, width), jnp.float32),
            pltpu.SemaphoreType.DMA((steps,)),
        ],
        compiler_params=room(*like(own, own, own, *blocks), ((width, width), jnp.float32)),
        cost_estimate=pl.CostEstimate(
            flops=2 * tokens * rows * width,
            bytes_accessed=4 * rows * width + 4 * tokens * width,
            transcendentals=0,
        ),
        name="far_tile",
    )(shrink, own, *blocks)


def behind(block, k):
    count = lax.axis_size("feat")
    return lax.ppermute(block, "feat", [((i + 2 * k) % count, i) for i in range(count)])


def swapped(block):
    return lax.ppermute(block, "feat", [(i, i ^ 1) for i in range(lax.axis_size("feat"))])


def shards(acts, layer_order, groups, group_scale, shrink):
    layers, _, _ = acts.shape
    half = lax.axis_size("feat") // 2
    chips = half
    reach = chips // 2

    sent = select(acts, layer_order)
    blocks = [sent[0]]
    for k in range(1, layers):
        route = [(i, partner(i, k, layers)) for i in range(layers)]
        blocks.append(lax.ppermute(sent[k], "layer", route))

    parts = [join(blocks[:1]), join(blocks[1:-1]), join(blocks[-1:])]
    ahead = [parts]
    for k in range(1, reach + 1):
        if k == 2:
            parts = [join(parts[:-1]), parts[-1]]
        moved = []
        for block in parts:
            moved.append(behind(block, 1))
        parts = moved
        ahead.append(parts)

    first, gains = prepare(blocks[0], groups, group_scale)
    own, part = gather([first, *blocks[1:]])
    part = part + swapped(part)
    sums = [part]
    for k in range(1, chips):
        sums.append(behind(part, k))
    stack = None
    for k in range(1, reach):
        stack, panel = tile(stack, half, own, ahead[k], lambda core, k=k: 2 * k, shrink, keep=True)
        other = swapped(panel)
        if k == reach - 1:
            stack = tile(stack, half, own, [own], lambda core: 0, shrink, diagonal=[gains, *sums])
        index = lambda core, k=k: jnp.where(core == 0, 2 * k + 1, 2 * k - 1)
        stack = tile(stack, half, own, [other], index, shrink)
    other = swapped(own)
    odd = []
    for block in ahead[reach]:
        odd.append(swapped(block))
    far = far_tile(own, ahead[reach], shrink)
    index = lambda core: jnp.where(core == 0, 1, half - 1)
    stack = tile(stack, half, own, [other], index, shrink, odd=odd)
    return (stack[None, None], far[None, None])


def solution(mesh):
    placed = (P(None, "layer", "feat"), P("layer", None), P("feat"), P("layer", None), P("layer"))

    return jax.shard_map(
        shards,
        mesh=mesh,
        in_specs=placed,
        out_specs=(P("layer", "feat", None, None, None), P("layer", "feat", None, None)),
        check_vma=False,
    )
```

```python
import math

import jax
import jax.numpy as jnp
from jax import lax
from jax.experimental import pallas as pl
from jax.experimental.pallas import tpu as pltpu
from jax.sharding import PartitionSpec as P

TRANSPOSED = (((0,), (0,)), ((), ()))
SMEM = pl.BlockSpec(memory_space=pltpu.SMEM)
VMEM = pl.BlockSpec(memory_space=pltpu.VMEM)
HBM = pl.BlockSpec(memory_space=pltpu.HBM)
ANY = pl.BlockSpec(memory_space=pl.ANY)


def room(*shapes):
    total = sum(math.prod(shape) * jnp.dtype(dtype).itemsize for shape, dtype in shapes)
    return pltpu.CompilerParams(vmem_limit_bytes=total + (2 << 20))


def like(*arrays):
    return [(a.shape, a.dtype) for a in arrays]


def partner(i, k, count):
    return (i + k) % count if count & (count - 1) else i ^ k


def select(acts, layer_order):
    layers, rows, width = acts.shape

    def body(order_ref, acts_ref, *rest):
        outs, (held, order, sem) = rest[:layers], rest[layers:]
        copies = [
            pltpu.make_async_copy(order_ref, order, sem.at[0]),
            pltpu.make_async_copy(acts_ref, held, sem.at[1]),
        ]
        for copy in copies:
            copy.start()
        here = lax.axis_index("layer")
        copies[0].wait()
        slots = []
        for k in range(layers):
            layer = partner(here, k, layers)
            slot = jnp.int32(0)
            for s in range(1, layers):
                slot = jnp.where(order[0, s] == layer, s, slot)
            slots.append(slot)
        copies[1].wait()
        outs[0][:rows, :] = held[slots[0]]
        outs[0][rows:, :] = held[slots[1]]
        for out, slot in zip(outs[1:], slots[1:]):
            out[...] = held[slot]

    return pl.pallas_call(
        body,
        out_shape=[jax.ShapeDtypeStruct((2 * rows, width), acts.dtype)]
        + [jax.ShapeDtypeStruct((rows, width), acts.dtype)] * (layers - 1),
        in_specs=[ANY, ANY],
        out_specs=[VMEM] * layers,
        scratch_shapes=[
            pltpu.VMEM(acts.shape, acts.dtype),
            pltpu.SMEM(layer_order.shape, layer_order.dtype),
            pltpu.SemaphoreType.DMA((2,)),
        ],
        name="select",
    )(layer_order, acts)


def prepare(block, rows, groups, group_scale):
    count = group_scale.shape[1]
    line = (1, groups.shape[0])

    def body(scale_hbm, groups_hbm, block_hbm, out_ref, gains_ref, scale, held, sem):
        copies = [
            pltpu.make_async_copy(scale_hbm, scale, sem.at[0]),
            pltpu.make_async_copy(groups_hbm, held, sem.at[1]),
            pltpu.make_async_copy(block_hbm.at[pl.ds(0, rows), :], out_ref, sem.at[2]),
        ]
        for copy in copies:
            copy.start()
        for copy in copies:
            copy.wait()
        value = jnp.zeros(line, jnp.float32)
        for g in range(count):
            value = jnp.where(held[...] == g, scale[0, g], value)
        gains_ref[...] = value

    return pl.pallas_call(
        body,
        out_shape=[
            jax.ShapeDtypeStruct((rows, block.shape[1]), block.dtype),
            jax.ShapeDtypeStruct(line, jnp.float32),
        ],
        in_specs=[ANY] * 3,
        out_specs=[VMEM] * 2,
        scratch_shapes=[
            pltpu.SMEM(group_scale.shape, group_scale.dtype),
            pltpu.VMEM(line, groups.dtype),
            pltpu.SemaphoreType.DMA((3,)),
        ],
        compiler_params=room(*like(block, block, groups, groups)),
        name="prepare",
    )(group_scale, groups[None], block)


def join(*pieces):
    if len(pieces) == 1 and pieces[0][2] == pieces[0][0].shape[0]:
        return pieces[0][0]
    total = sum(rows for _, _, rows in pieces)
    arrays = [piece[0] for piece in pieces]
    width, dtype = arrays[0].shape[1], arrays[0].dtype

    def body(*refs):
        at = 0
        for ref, (_, start, rows) in zip(refs, pieces):
            refs[-1][at : at + rows, :] = ref[start : start + rows, :]
            at += rows

    return pl.pallas_call(
        body,
        out_shape=jax.ShapeDtypeStruct((total, width), dtype),
        in_specs=[VMEM] * len(arrays),
        out_specs=VMEM,
        compiler_params=room(*like(*arrays), ((total, width), dtype)),
        name="join",
    )(*arrays)


def chip_trace(own, other):
    tokens = own.shape[0]

    def body(own_ref, other_ref, out_ref):
        total = jnp.zeros((1, own.shape[1]), jnp.float32)
        for ref in (own_ref, other_ref):
            value = ref[...].astype(jnp.float32)
            total = total + jnp.sum(value * value, axis=0, keepdims=True)
        out_ref[...] = jnp.broadcast_to(jnp.sum(total) / tokens, out_ref.shape)

    return pl.pallas_call(
        body,
        out_shape=jax.ShapeDtypeStruct((8, 128), jnp.float32),
        in_specs=[VMEM] * 2,
        out_specs=VMEM,
        compiler_params=room(*like(own, other)),
        name="chip_trace",
    )(own, other)


def place():
    f = lax.axis_index("feat")
    return f, f // 2, f % 2


def assemble(panel_ref, blocks):
    start = 0
    for block in blocks:
        panel_ref[start : start + block.shape[0], :] = block[...]
        start += block.shape[0]


def fill(stack, count, own, tasks, shrink, keep=False, patch=()):
    tokens, width = own.shape
    given = [block for even, odd, _ in tasks for block in (*even, *odd)]
    step = next(s for s in (128, 64, 32, 16, 8, width) if width % s == 0)
    steps = width // step
    lines = [slice(i * step, (i + 1) * step) for i in range(steps)]

    def body(shrink_ref, own_ref, *rest):
        parts, rest = rest[: len(given)], rest[len(given) :]
        added, rest = rest[: len(patch)], rest[len(patch) :]
        rest = rest[(stack is not None) :]
        out_ref, rest = rest[0], rest[1:]
        if keep:
            corner_ref, rest = rest[0], rest[1:]
        panel, buffer, fixed, sem = rest
        _, _, core = place()
        scale = (1.0 - shrink_ref[0]) * (1.0 / tokens)
        copies = []

        def write(source, target):
            copies.append(pltpu.make_async_copy(source, target, sem.at[len(copies)]))
            copies[-1].start()

        for t, (even, odd, index) in enumerate(tasks):
            first, parts = parts[: len(even)], parts[len(even) :]
            second, parts = parts[: len(odd)], parts[len(odd) :]
            if odd:
                pl.when(core == 0)(lambda first=first: assemble(panel, first))
                pl.when(core != 0)(lambda second=second: assemble(panel, second))
            else:
                assemble(panel, first)
            to = index(core)
            for rows in lines:
                value = lax.dot_general(
                    own_ref[:, rows],
                    panel[...],
                    TRANSPOSED,
                    preferred_element_type=jnp.float32,
                )
                value = value * scale
                buffer[t, rows, :] = value
                if keep and t == len(tasks) - 1:
                    corner_ref[rows, :] = value[:, rows]
                write(buffer.at[t, rows, :], out_ref.at[to, rows, :])
        if patch:
            corner, gains_ref, sums = added[0], added[1], added[2:]
            trace = sums[0][0:1, 0:1]
            for other in sums[1:]:
                trace = trace + other[0:1, 0:1]
            mu = trace * (1.0 / (width * lax.axis_size("feat")))
            line = gains_ref[...] * (mu * shrink_ref[0])
            same = lax.broadcasted_iota(jnp.int32, (step, step), 0) == lax.broadcasted_iota(
                jnp.int32, (step, step), 1
            )
            for rows in lines:
                fixed[rows, :] = corner[rows, :] + jnp.where(same, line[:, rows], 0.0)
                write(fixed.at[rows, :], out_ref.at[0, rows, rows])
        for copy in copies:
            copy.wait()

    out_shape = [jax.ShapeDtypeStruct((count, width, width), jnp.float32)]
    out_specs = [ANY]
    if keep:
        out_shape.append(jax.ShapeDtypeStruct((width, step), jnp.float32))
        out_specs.append(VMEM)
    held = ((len(tasks) + 1, width, width), jnp.float32)
    operands = [shrink, own, *given, *patch] + ([] if stack is None else [stack])
    in_specs = [SMEM] + [VMEM] * (1 + len(given) + len(patch)) + [ANY] * (stack is not None)
    outs = pl.pallas_call(
        body,
        out_shape=out_shape,
        in_specs=in_specs,
        out_specs=out_specs,
        scratch_shapes=[
            pltpu.VMEM((tokens, width), own.dtype),
            pltpu.VMEM((len(tasks), width, width), jnp.float32),
            pltpu.VMEM((width, step), jnp.float32),
            pltpu.SemaphoreType.DMA((steps * (len(tasks) + 1),)),
        ],
        input_output_aliases={} if stack is None else {len(operands) - 1: 0},
        compiler_params=room(*like(own, own, *given, *patch), held),
        cost_estimate=pl.CostEstimate(
            flops=2 * tokens * width * width * len(tasks),
            bytes_accessed=(4 * width * width + 4 * tokens * width) * len(tasks),
            transcendentals=0,
        ),
        name="gram_tiles",
    )(*operands)
    return outs if keep else outs[0]


def far_tile(own, blocks, shrink):
    tokens, width = own.shape
    rows = width // 2

    step = next(s for s in (128, 64, 32, 16, 8, rows) if rows % s == 0)
    steps = rows // step

    def body(shrink_ref, own_ref, *rest):
        parts, (out_ref, left, panel, buffer, sem) = rest[: len(blocks)], rest[len(blocks) :]
        f, _, _ = place()
        lower = f < lax.axis_size("feat") // 2
        scale = (1.0 - shrink_ref[0]) * (1.0 / tokens)
        assemble(panel, parts)

        @pl.when(lower)
        def _():
            left[...] = own_ref[:, :rows]

        @pl.when(jnp.logical_not(lower))
        def _():
            left[...] = panel[:, rows:]
            panel[...] = own_ref[...]

        copies = []
        for i in range(steps):
            part = slice(i * step, (i + 1) * step)
            buffer[part, :] = (
                lax.dot_general(
                    left[:, part],
                    panel[...],
                    TRANSPOSED,
                    preferred_element_type=jnp.float32,
                )
                * scale
            )
            copies.append(
                pltpu.make_async_copy(buffer.at[part, :], out_ref.at[part, :], sem.at[i])
            )
            copies[-1].start()
        for copy in copies:
            copy.wait()

    return pl.pallas_call(
        body,
        out_shape=jax.ShapeDtypeStruct((rows, width), jnp.float32),
        in_specs=[SMEM] + [VMEM] * (1 + len(blocks)),
        out_specs=ANY,
        scratch_shapes=[
            pltpu.VMEM((tokens, rows), own.dtype),
            pltpu.VMEM((tokens, width), own.dtype),
            pltpu.VMEM((rows, width), jnp.float32),
            pltpu.SemaphoreType.DMA((steps,)),
        ],
        compiler_params=room(*like(own, own, own, *blocks), ((width, width), jnp.float32)),
        cost_estimate=pl.CostEstimate(
            flops=2 * tokens * rows * width,
            bytes_accessed=4 * rows * width + 4 * tokens * width,
            transcendentals=0,
        ),
        name="far_tile",
    )(shrink, own, *blocks)


def behind(block, k):
    count = lax.axis_size("feat")
    return lax.ppermute(block, "feat", [((i + 2 * k) % count, i) for i in range(count)])


def paired(block, k):
    chips = lax.axis_size("feat") // 2
    pairs = [(z, partner(z, k, chips)) for z in range(chips)]
    return lax.ppermute(block, "feat", [(2 * s + c, 2 * d + c) for s, d in pairs for c in (0, 1)])


def swapped(block):
    return lax.ppermute(block, "feat", [(i, i ^ 1) for i in range(lax.axis_size("feat"))])


def shards(acts, layer_order, groups, group_scale, shrink):
    layers, _, _ = acts.shape
    half = lax.axis_size("feat") // 2
    chips = half
    reach = chips // 2

    pair, *sent = select(acts, layer_order)
    rows = acts.shape[1]

    def exchanged(block, k):
        route = [(i, partner(i, k, layers)) for i in range(layers)]
        return lax.ppermute(block, "layer", route)

    def onward(block):
        return behind(block, 1)

    got = [exchanged(block, k + 1) for k, block in enumerate(sent)]
    first, gains = prepare(pair, rows, groups, group_scale)

    near = onward(pair)
    middle = join(*[(block, 0, rows) for block in got[1:-1]])
    middle_near = onward(middle)
    last_near = onward(got[-1])
    crossed = exchanged(join((near, rows, rows)), 1)
    parts = [
        join((near, 0, rows), (middle_near, 0, middle.shape[0])),
        join((crossed, 0, rows), (last_near, 0, rows)),
    ]
    ahead = [None, parts]
    for _ in range(2, reach + 1):
        parts = [onward(block) for block in parts]
        ahead.append(parts)

    own = join(*[(block, 0, block.shape[0]) for block in (first, middle, got[0], got[-1])])
    beside = swapped(own)
    stack, corner = fill(None, half, own, [([own], (), lambda core: 0)], shrink, keep=True)
    part = chip_trace(own, beside)
    sums = [part]
    for k in range(1, chips):
        sums.append(paired(part, k))
    tasks = []
    for k in range(1, reach):
        other = []
        for block in ahead[k]:
            other.append(swapped(block))
        tasks.append((ahead[k], (), lambda core, k=k: 2 * k))
        tasks.append((other, (), lambda core, k=k: jnp.where(core == 0, 2 * k + 1, 2 * k - 1)))
    for t in range(0, len(tasks), 2):
        stack = fill(stack, half, own, tasks[t : t + 2], shrink)
    odd = []
    for block in ahead[reach]:
        odd.append(swapped(block))
    far = far_tile(own, ahead[reach], shrink)
    index = lambda core: jnp.where(core == 0, 1, half - 1)
    patch = [corner, gains, *sums]
    stack = fill(stack, half, own, [([beside], odd, index)], shrink, patch=patch)
    return (stack[None, None], far[None, None])


def solution(mesh):
    placed = (P(None, "layer", "feat"), P("layer", None), P("feat"), P("layer", None), P("layer"))

    return jax.shard_map(
        shards,
        mesh=mesh,
        in_specs=placed,
        out_specs=(P("layer", "feat", None, None, None), P("layer", "feat", None, None)),
        check_vma=False,
    )
```
